128 devices in a mesh: ctx: 64 (over z, y, x_hi, core), chan: 2 (over x_lo).
Axes of the slice: x: 4 (x_hi: 2, x_lo: 2; x = x_hi * 2 + x_lo), y: 4, z: 4, core: 2. Of those that a mesh axis runs over, the one named last changes fastest.
Arguments:
- hidden: bfloat16 [16384, 2048], P('ctx'), may hold values from -6 to 6
- in_weight: bfloat16 [2048, 4096], P(None, 'chan'), may hold values from -0.125 to 0.125
- state_proj: bfloat16 [2, 16384, 128], P(None, 'ctx'), may hold values from -2.09375 to 2.09375
- log_decay: float32 [2, 16384, 64], P(None, 'ctx', 'chan'), may hold values from -1.6 to 0, as said below
- step_size: float32 [2, 16384, 64], P(None, 'ctx', 'chan'), may hold values from 0 to 1, as said below
- skip_gain: float32 [64], P('chan'), may hold values from 0.1 to 1.9
- cotangent: bfloat16 [16384, 4096], P('ctx', 'chan'), may hold values from -6 to 6
Outputs:
- layer_out: bfloat16 [16384, 4096], P('ctx', 'chan')
- input_grad: bfloat16 [16384, 2048], P('ctx', 'chan')
The draws below stay inside these ranges and needn't reach their ends.
Inputs may be any that keep to these rules, and one draw needn't show every extreme that they name: log_decay is never positive. step_size is positive.
All inputs are finite; a program needn't handle non-finite values.
Results may differ from the reference program's by a relative error of at most 0.014.
Values may be sent and summed in bfloat16 or wider, within the bound.
No kernel may reach another device: no remote copies, remote signals or barrier semaphores. Data moves between devices by JAX's collectives and lax.ppermute only.
A program may use at most 640 MiB of HBM per device.

```python
import math
import jax
import jax.numpy as jnp
from jax import lax

D = 2048
HEAD_TOTAL = 64
HEAD_DIM = 64
STATE = 64
GROUP = 128
TOK_DEV = 256
TOKEN_LENGTH = 16384
INNER = 4096


def selective_laws(key):
    random_keys = jax.random.split(jax.random.fold_in(key, 29), 8)
    fast_share = 0.3
    middle_top = 1.0 / 30.0
    choose = jax.random.uniform(random_keys[0], (2, HEAD_TOTAL))
    fast_base = jnp.exp(jax.random.uniform(random_keys[1], (2, HEAD_TOTAL), minval=math.log(1.0 / 50.0), maxval=math.log(1.0 / 30.0)))
    middle_base = jnp.exp(jax.random.uniform(random_keys[2], (2, HEAD_TOTAL), minval=math.log(0.01 / TOKEN_LENGTH), maxval=math.log(middle_top)))
    base_rate = jnp.where(choose < fast_share, fast_base, middle_base)
    block_count = TOKEN_LENGTH // TOK_DEV
    block_factor = jnp.exp(jax.random.uniform(random_keys[3], (2, block_count, 1, HEAD_TOTAL), minval=math.log(0.5), maxval=math.log(2.0)))
    block_factor = jnp.broadcast_to(block_factor, (2, block_count, TOK_DEV, HEAD_TOTAL)).reshape(2, TOKEN_LENGTH, HEAD_TOTAL)
    roughness = jnp.exp(jax.random.uniform(random_keys[4], (2, TOKEN_LENGTH, HEAD_TOTAL), minval=math.log(0.5), maxval=math.log(2.0)))
    decay_speed = base_rate[:, None, :] * block_factor * roughness
    spike_position = jax.random.randint(random_keys[5], (2, 2), 0, TOKEN_LENGTH)
    token_positions = jnp.arange(TOKEN_LENGTH)
    spike_events = jnp.sum((token_positions[None, None, :] == spike_position[:, :, None]).astype(jnp.float32), axis=1)
    spike_loss = jax.random.uniform(random_keys[6], (2, HEAD_TOTAL), minval=0.22, maxval=0.69)
    decay_values = -decay_speed - spike_events[:, :, None] * spike_loss[:, None, :]
    step_rough = jnp.exp(jax.random.uniform(random_keys[7], (2, TOKEN_LENGTH, HEAD_TOTAL), minval=math.log(0.7), maxval=math.log(1.4)))
    step_sizes = jnp.sqrt(2.0 * decay_speed + 4.0 / TOKEN_LENGTH) * step_rough
    return (decay_values.astype(jnp.float32), step_sizes.astype(jnp.float32))


def draw_log_decay(key, part):
    return selective_laws(key)[0]


def draw_step_size(key, part):
    return selective_laws(key)[1]


def steps_of(stream_key, extent, shards, least, high):
    gain, own = 1.0, jax.random.fold_in(stream_key, 6)
    for position, blocks in shards:
        steps = jnp.exp(jax.random.uniform(jax.random.fold_in(own, position), (blocks,), jnp.float32, least / len(shards), high / len(shards)))
        gain = gain * jnp.repeat(steps, extent[position] // blocks).reshape([-1 if axis == position else 1 for axis in range(len(extent))])
    return gain


def scatter_about(key, extent, deviation, reach, shards=(), held_as=jnp.bfloat16):
    level = steps_of(key, extent, shards, -0.22, 0.18) if shards else 1.0
    entries = jax.random.normal(key, extent, jnp.float32) * deviation * level
    return jnp.minimum(jnp.maximum(entries, -reach), reach).astype(held_as)


def setup_inputs(seed: int = 0) -> dict:
    arg_keys = jax.random.split(jax.random.key(seed), 8)
    hidden = scatter_about(arg_keys[0], (TOKEN_LENGTH, D), 1.0, 6.0, ((0, 64),))
    in_weight = scatter_about(arg_keys[1], (D, INNER), D ** -0.5, 0.125, ((1, 2),))
    state_proj = scatter_about(arg_keys[2], (2, TOKEN_LENGTH, 2 * STATE), 0.35, 2.09375, ((1, 64),))
    log_decay = draw_log_decay(jax.random.fold_in(arg_keys[7], 71), 0)
    step_size = draw_step_size(jax.random.fold_in(arg_keys[7], 71), 0)
    skip_gain = jnp.clip(1.0 + 0.18 * jax.random.normal(arg_keys[5], (HEAD_TOTAL,), jnp.float32), 0.1, 1.9)
    cotangent = scatter_about(arg_keys[6], (TOKEN_LENGTH, INNER), 1.0, 6.0, ((0, 64), (1, 2)))
    return {"hidden": hidden, "in_weight": in_weight, "state_proj": state_proj, "log_decay": log_decay, "step_size": step_size, "skip_gain": skip_gain, "cotangent": cotangent}


def block_scan(query_rows, key_rows, value_rows, weights, decay_values, exclusive):
    length = query_rows.shape[0]
    blocks = length // GROUP
    head_count = value_rows.shape[1]
    head_width = value_rows.shape[2]
    state_width = query_rows.shape[1]

    def advance(states, members):
        query_blk, key_blk, value_blk, weight_blk, decay_blk = members
        cumul = jnp.cumsum(decay_blk, axis=0)
        if exclusive:
            level = cumul - decay_blk
        else:
            level = cumul
        affinity = jnp.dot(query_blk, key_blk.T, preferred_element_type=jnp.float32)
        differ = level.T[:, :, None] - level.T[:, None, :]
        row_index = lax.broadcasted_iota(jnp.int32, (GROUP, GROUP), 0)
        col_index = lax.broadcasted_iota(jnp.int32, (GROUP, GROUP), 1)
        kernel = jnp.exp(jnp.where((row_index >= col_index)[None], differ, -jnp.inf))
        mixing = (affinity[None] * kernel * weight_blk.T[:, None, :]).astype(jnp.bfloat16)
        within = jnp.einsum("hts,shp->thp", mixing.astype(jnp.float32), value_blk.astype(jnp.float32), precision=lax.Precision.HIGHEST)
        rounded = states.astype(jnp.bfloat16).astype(jnp.float32)
        carried = jnp.exp(level)[:, :, None] * jnp.einsum("tn,hpn->thp", query_blk.astype(jnp.float32), rounded, precision=lax.Precision.HIGHEST)
        closing = cumul[-1]
        fading = jnp.exp(closing[None, :] - level) * weight_blk
        weighted = (fading[:, :, None] * key_blk.astype(jnp.float32)[:, None, :]).astype(jnp.bfloat16).astype(jnp.float32)
        states = jnp.exp(closing)[:, None, None] * states + jnp.einsum("shn,shp->hpn", weighted, value_blk.astype(jnp.float32), precision=lax.Precision.HIGHEST)
        return states, within + carried

    members = tuple(member.reshape((blocks, GROUP) + member.shape[1:]) for member in (query_rows, key_rows, value_rows, weights, decay_values))
    initial = jnp.zeros((head_count, head_width, state_width), jnp.float32)
    _, results = lax.scan(advance, initial, members)
    return results.reshape(length, head_count, head_width)


def reverse_rows(array):
    return jnp.flip(array, 0)


def reference(hidden, in_weight, state_proj, log_decay, step_size, skip_gain, cotangent):
    length = hidden.shape[0]
    u_fwd = jnp.dot(hidden, in_weight, preferred_element_type=jnp.float32).astype(jnp.bfloat16)
    u_rev = jnp.dot(hidden[:, ::-1], in_weight, preferred_element_type=jnp.float32).astype(jnp.bfloat16)
    keys_f = state_proj[0, :, :STATE]
    query_f = state_proj[0, :, STATE:]
    keys_r = state_proj[1, :, :STATE]
    query_r = state_proj[1, :, STATE:]
    gains = skip_gain[None, :, None]
    fwd_values = u_fwd.reshape(length, HEAD_TOTAL, HEAD_DIM)
    rev_values = u_rev.reshape(length, HEAD_TOTAL, HEAD_DIM)
    scan_ff = block_scan(query_f, keys_f, fwd_values, step_size[0], log_decay[0], False)
    y_fwd = scan_ff + gains * fwd_values.astype(jnp.float32)
    scan_rf = reverse_rows(block_scan(reverse_rows(query_r), reverse_rows(keys_r), reverse_rows(rev_values), reverse_rows(step_size[1]), reverse_rows(log_decay[1]), False))
    y_rev = (scan_rf + gains * rev_values.astype(jnp.float32)).astype(jnp.bfloat16)
    layer_out = (y_fwd.reshape(length, INNER) + y_rev.reshape(length, INNER)[:, ::-1].astype(jnp.float32)).astype(jnp.bfloat16)
    cot_values = cotangent.reshape(length, HEAD_TOTAL, HEAD_DIM)
    rc_cotangent = cotangent[:, ::-1].reshape(length, HEAD_TOTAL, HEAD_DIM)
    unit = jnp.ones_like(step_size[0])
    scan_fb = reverse_rows(block_scan(reverse_rows(keys_f), reverse_rows(query_f), reverse_rows(cot_values), unit, reverse_rows(log_decay[0]), True))
    grad_f = (step_size[0][:, :, None] * scan_fb + gains * cot_values.astype(jnp.float32)).astype(jnp.bfloat16)
    scan_rb = block_scan(keys_r, query_r, rc_cotangent, unit, log_decay[1], True)
    grad_r = (step_size[1][:, :, None] * scan_rb + gains * rc_cotangent.astype(jnp.float32)).astype(jnp.bfloat16)
    direct = jnp.dot(grad_f.reshape(length, INNER), in_weight.T, preferred_element_type=jnp.float32)
    mirrored = jnp.dot(grad_r.reshape(length, INNER), in_weight.T, preferred_element_type=jnp.float32)
    input_grad = (direct + mirrored[:, ::-1]).astype(jnp.bfloat16)
    return layer_out, input_grad
```

```python
import functools

import jax
import jax.numpy as jnp
from jax import lax
from jax.experimental import pallas as pl
from jax.experimental.pallas import tpu as pltpu
from jax.sharding import PartitionSpec as P

HEAD_DIM = 64
STATE = 64
TILE = 128
F32 = jnp.float32
BF16 = jnp.bfloat16
HIGHEST = lax.Precision.HIGHEST
SWAP = [(0, 1), (1, 0)]
EVERY = ("ctx", "chan")


def flip(array):
    return array[:, ::-1]


def within_kernel(upper, q_ref, k_ref, col_ref, row_ref, v_ref, o_ref, g_ref):
    rows = q_ref.shape[0]
    tiles = rows // TILE

    @pl.when(pl.program_id(0) == 0)
    def _():
        g = lax.dot_general(
            q_ref[...], k_ref[...], (((1,), (1,)), ((), ())), preferred_element_type=F32
        )
        t = lax.broadcasted_iota(jnp.int32, g.shape, 0)
        s = lax.broadcasted_iota(jnp.int32, g.shape, 1)
        keep = (t <= s) if upper else (t >= s)
        g_ref[...] = jnp.where(keep, g, 0.0)

    lane = lax.broadcasted_iota(jnp.int32, (TILE, 2 * HEAD_DIM), 1)
    for i in range(tiles):
        span = range(i, tiles) if upper else range(i + 1)
        first, last = span[0] * TILE, (span[-1] + 1) * TILE
        v = v_ref[first:last, :]
        outs = []
        for h in range(2):
            level_t = col_ref[0, i * TILE : (i + 1) * TILE, h : h + 1]
            level_s = row_ref[0, h : h + 1, first:last]
            mixing = g_ref[i * TILE : (i + 1) * TILE, first:last] * jnp.exp(
                jnp.minimum(level_t - level_s, 0.0)
            )
            outs.append(jnp.dot(mixing.astype(BF16), v, preferred_element_type=F32))
        o_ref[i * TILE : (i + 1) * TILE, :] = jnp.where(lane < HEAD_DIM, outs[0], outs[1])


def within(upper, query, key, level, values):
    rows, inner = values.shape
    pairs = inner // (2 * HEAD_DIM)
    columns = level.reshape(rows, pairs, 2).transpose(1, 0, 2)
    across = level.T.reshape(pairs, 2, rows)
    return pl.pallas_call(
        functools.partial(within_kernel, upper),
        out_shape=jax.ShapeDtypeStruct((rows, inner), F32),
        grid=(pairs,),
        in_specs=[
            pl.BlockSpec((rows, STATE), lambda i: (0, 0)),
            pl.BlockSpec((rows, STATE), lambda i: (0, 0)),
            pl.BlockSpec((1, rows, 2), lambda i: (i, 0, 0)),
            pl.BlockSpec((1, 2, rows), lambda i: (i, 0, 0)),
            pl.BlockSpec((rows, 2 * HEAD_DIM), lambda i: (0, i)),
        ],
        out_specs=pl.BlockSpec((rows, 2 * HEAD_DIM), lambda i: (0, i)),
        scratch_shapes=[pltpu.VMEM((rows, rows), F32)],
        cost_estimate=pl.CostEstimate(
            flops=4 * rows * rows * inner,
            bytes_accessed=6 * rows * inner,
            transcendentals=rows * rows * pairs * 2,
        ),
        name="within",
    )(query, key, columns, across, values)


def carry_kernel(perm_ref, r_ref, e_ref, o_ref, s_ref, a_ref, c_ref):
    wide = o_ref.shape[1]
    half = wide // 2
    units = e_ref.shape[0]
    groups = r_ref.shape[0] // 8
    s_ref[...] = jnp.dot(perm_ref[...], r_ref[:, :wide], preferred_element_type=F32)
    decay = jnp.dot(
        perm_ref[...], r_ref[:, wide : wide + 2 * units], preferred_element_type=F32
    ).astype(BF16)
    a_ref[...] = jnp.dot(
        decay[:, :units], e_ref[...], preferred_element_type=F32
    ) + jnp.dot(decay[:, units:], e_ref[...], preferred_element_type=F32)

    def group(g, both):
        ahead, back = both
        low = pl.ds(pl.multiple_of(8 * g, 8), 8)
        high = pl.ds(pl.multiple_of(8 * (groups - 1 - g), 8), 8)
        decays, states = a_ref[low, :half], s_ref[low, :half]
        held = []
        for i in range(4):
            held.append(ahead)
            rows = slice(2 * i, 2 * i + 2)
            ahead = decays[rows] * ahead + states[rows]
        c_ref[low, :half] = jnp.concatenate(held, axis=0)
        decays, states = a_ref[high, half:], s_ref[high, half:]
        held = []
        for i in range(3, -1, -1):
            held.insert(0, back)
            rows = slice(2 * i, 2 * i + 2)
            back = decays[rows] * back + states[rows]
        c_ref[high, half:] = jnp.concatenate(held, axis=0)
        return ahead, back

    zero = jnp.zeros((2, half), F32)
    lax.fori_loop(0, groups, group, (zero, zero))
    o_ref[...] = c_ref[...].astype(BF16)


def carried(perm, gathered, expand):
    rows = gathered.shape[0]
    wide = expand.shape[1]
    return pl.pallas_call(
        carry_kernel,
        out_shape=jax.ShapeDtypeStruct((rows, wide), BF16),
        scratch_shapes=[pltpu.VMEM((rows, wide), F32)] * 3,
        name="carried",
    )(perm, gathered, expand)


def split_two(x):
    high = lax.reduce_precision(x, 8, 7)
    return high.astype(BF16), (x - high).astype(BF16)


def shards(hidden, in_weight, state_proj, log_decay, step_size, skip_gain, cotangent):
    rows, depth = hidden.shape
    heads = skip_gain.shape[0]
    inner = heads * HEAD_DIM
    chan = lax.axis_index("chan")
    keys_f, query_f = state_proj[0, :, :STATE], state_proj[0, :, STATE:]
    keys_r, query_r = state_proj[1, :, :STATE], state_proj[1, :, STATE:]
    decay_f, decay_r = log_decay[0], log_decay[1]
    step_f, step_r = step_size[0], step_size[1]

    other = lax.ppermute(
        jnp.concatenate([decay_r, step_r, jnp.broadcast_to(skip_gain, (8, heads))]), "chan", SWAP
    )
    far_decay, far_step, far_skip = other[:rows], other[rows : 2 * rows], other[2 * rows]
    cot_mirror = flip(cotangent)
    g_r = lax.ppermute(cot_mirror, "chan", SWAP)

    u_rev = jnp.dot(flip(hidden), in_weight, preferred_element_type=F32).astype(BF16)
    u_mirror = flip(u_rev)
    v_r = lax.ppermute(u_mirror, "chan", SWAP)
    u_f = jnp.dot(hidden, in_weight, preferred_element_type=F32).astype(BF16)

    spread = (
        lax.broadcasted_iota(jnp.int32, (heads, inner), 1) // HEAD_DIM
        == lax.broadcasted_iota(jnp.int32, (heads, inner), 0)
    ).astype(F32)
    spread_two = (
        lax.broadcasted_iota(jnp.int32, (2 * heads, 2 * inner), 1) // HEAD_DIM
        == lax.broadcasted_iota(jnp.int32, (2 * heads, 2 * inner), 0)
    ).astype(BF16)

    def wide(x):
        return jnp.dot(x, spread, precision=HIGHEST, preferred_element_type=F32)

    triangle = (
        lax.broadcasted_iota(jnp.int32, (rows, rows), 0)
        >= lax.broadcasted_iota(jnp.int32, (rows, rows), 1)
    ).astype(F32)
    decays = jnp.concatenate(
        [decay_f, flip(decay_r), decay_r, far_decay, flip(far_decay)], axis=1
    )
    sums = jnp.dot(triangle, decays, precision=HIGHEST, preferred_element_type=F32)
    sum_f, sum_m, sum_r, sum_far, sum_farm = jnp.split(sums, 5, axis=1)
    dec_f, dec_m, dec_r, dec_far, dec_farm = jnp.split(decays, 5, axis=1)

    def state(key, weight, values):
        scaled = (wide(weight) * values.astype(F32)).astype(BF16)
        return lax.dot_general(
            key, scaled, (((0,), (0,)), ((), ())), preferred_element_type=F32
        ).astype(BF16)

    state_ff = state(keys_f, jnp.exp(sum_f[-1:] - sum_f) * step_f, u_f)
    state_fb = state(query_f, jnp.exp(sum_f), cotangent)
    state_rb = state(query_r, jnp.exp(sum_far[-1:] - sum_far + dec_far), cot_mirror)
    state_rf = state(keys_r, jnp.exp(sum_m - dec_m) * flip(step_r), u_mirror)

    def fade(one, two):
        pair = jnp.exp(jnp.concatenate([one[-1:], two[-1:]], axis=1))
        high, low = split_two(pair)
        return jnp.broadcast_to(jnp.concatenate([high, low], axis=1), (STATE, 4 * heads))

    outgoing = jnp.stack(
        [
            jnp.concatenate([state_ff, state_fb, fade(sum_f, sum_f)], axis=1),
            jnp.concatenate([state_rb, state_rf, fade(sum_far, sum_m)], axis=1),
        ],
        axis=1,
    ).reshape(2 * STATE, -1)
    gathered = lax.all_to_all(outgoing, EVERY, 0, 0, tiled=True)
    lines = gathered.shape[0]
    target = lax.broadcasted_iota(jnp.int32, (lines, lines), 0)
    source = lax.broadcasted_iota(jnp.int32, (lines, lines), 1)
    perm = (source == target + chan * (1 - 2 * (target % 2))).astype(BF16)
    returned = lax.all_to_all(carried(perm, gathered, spread_two), EVERY, 0, 0, tiled=True)
    returned = returned.reshape(STATE, 2, 2 * inner)
    carry_ff, carry_fb = returned[:, 0, :inner], returned[:, 0, inner:]
    carry_rb, carry_rf = returned[:, 1, :inner], returned[:, 1, inner:]

    level_ff = sum_f
    level_fb = sum_f[-1:] - sum_f
    level_rb = sum_r - dec_r
    level_rf = sum_farm[-1:] - sum_farm + dec_farm
    far_step = flip(far_step)
    far_gain = jnp.repeat(far_skip[::-1], HEAD_DIM)[None]
    gain = jnp.repeat(skip_gain, HEAD_DIM)[None]
    values_ff = (wide(step_f) * u_f.astype(F32)).astype(BF16)
    values_rf = (wide(far_step) * v_r.astype(F32)).astype(BF16)
    near_ff = within(False, query_f, keys_f, level_ff, values_ff)
    near_fb = within(True, keys_f, query_f, level_fb, cotangent)
    near_rb = within(False, keys_r, query_r, level_rb, g_r)
    near_rf = within(True, query_r, keys_r, level_rf, values_rf)

    def total(near, query, level, carry):
        far = jnp.dot(query, carry, preferred_element_type=F32)
        return near + wide(jnp.exp(level)) * far

    y_f = total(near_ff, query_f, level_ff, carry_ff) + gain * u_f.astype(F32)
    y_r = (total(near_rf, query_r, level_rf, carry_rf) + far_gain * v_r.astype(F32)).astype(BF16)
    layer_out = (y_f + y_r.astype(F32)).astype(BF16)
    du_f = (
        wide(step_f) * total(near_fb, keys_f, level_fb, carry_fb)
        + gain * cotangent.astype(F32)
    ).astype(BF16)
    du_r = (
        wide(step_r) * total(near_rb, keys_r, level_rb, carry_rb) + gain * g_r.astype(F32)
    ).astype(BF16)

    half = depth // 2
    mine = lax.dynamic_slice_in_dim(in_weight, chan * half, half, 0)
    theirs = lax.dynamic_slice_in_dim(in_weight, (1 - chan) * half, half, 0)

    def back(values, weight):
        return lax.dot_general(
            values, weight, (((1,), (1,)), ((), ())), preferred_element_type=F32
        )

    sent = (back(du_f, theirs) + flip(back(du_r, mine))).astype(BF16)
    arrived = lax.ppermute(sent, "chan", SWAP)
    kept = back(du_f, mine) + flip(back(du_r, theirs))
    return layer_out, (kept + arrived.astype(F32)).astype(BF16)


def solution(mesh):
    in_specs = (
        P("ctx", None),
        P(None, "chan"),
        P(None, "ctx", None),
        P(None, "ctx", "chan"),
        P(None, "ctx", "chan"),
        P("chan"),
        P("ctx", "chan"),
    )
    out_specs = (P("ctx", "chan"), P("ctx", "chan"))
    return jax.shard_map(shards, mesh=mesh, in_specs=in_specs, out_specs=out_specs, check_vma=False)
```
